512 devices in a mesh: section: 2 (over core), region: 256 (over z, y, x).
Axes of the slice: x: 4, y: 8, z: 8, core: 2. Of those that a mesh axis runs over, the one named last changes fastest.
Arguments:
- hits: bfloat16 [2, 65536, 512], P('section', 'region'), may hold values from -6 to 6
- order: int32 [2, 256, 256], P(None, 'region'), may hold values from 0 to 255, each once within a row
- links: int32 [2, 512, 3], P(None, 'region'), may hold values from 0 to 511, as said below
- counts: int32 [2, 256], replicated, may hold values from 64 to 256, as said below
- w_qkv: bfloat16 [2, 512, 1536], P('section')
- w_out: bfloat16 [2, 512, 512], P('section'), may hold values from -0.25 to 0.25
- w_up: bfloat16 [2, 512, 2048], P('section'), may hold values from -0.25 to 0.25
- w_down: bfloat16 [2, 2048, 512], P('section'), may hold values from -0.125 to 0.125
Outputs:
- encoded: bfloat16 [2, 65536, 512], P('section', 'region')
The draws below stay inside these ranges and needn't reach their ends.
Inputs may be any that keep to these rules, and one draw needn't show every extreme that they name: `links`: entry 0 of patch g is g itself; the other entries are distinct patches other than g, at most 2 patches away from g along the curve. `counts`: in every event some region is full and some region holds 64 hits. `order`: each region's entries along the last dimension list each of its 256 hits once.
All inputs are finite; a program needn't handle non-finite values.
Results may differ from the reference program's by a relative error of at most 0.015.
Values may be sent and summed in bfloat16 or wider, within the bound.
No kernel may reach another device: no remote copies, remote signals or barrier semaphores. Data moves between devices by JAX's collectives and lax.ppermute only.
A program may use at most 64 MiB of HBM per device.

```python
import jax
import jax.numpy as jnp
from jax import lax

D = 512
HEADS = 8
FF = 2048
HEAD_DIM = 64
PATCH = 128
REACH = 2
LINKS = 3
H_DEV = 256
BLOCKS = 2
MICRO = 2
REGIONS = 256
HITS = 65536
TOTAL_PATCHES = 512


def draw_links(key, part):
    slots = jnp.arange(2 * REACH)
    offsets = slots - REACH + (slots >= REACH).astype(jnp.int32)
    patches_all = jnp.arange(TOTAL_PATCHES)
    target = patches_all[None, :, None] + offsets[None, None, :]
    target = jnp.broadcast_to(target, (MICRO, TOTAL_PATCHES, 2 * REACH))
    raw = jax.random.randint(key, (MICRO, TOTAL_PATCHES, 2 * REACH), 0, 1 << 20)
    score = raw * (2 * REACH) + slots[None, None, :]
    inside = (target >= 0) & (target < TOTAL_PATCHES)
    score = jnp.where(inside, score, score - (1 << 24))
    chosen_score, picked = lax.top_k(score, LINKS - 1)
    chosen = jnp.take_along_axis(target, picked, axis=2)
    itself = jnp.broadcast_to(patches_all[None, :, None], (MICRO, TOTAL_PATCHES, 1))
    return jnp.concatenate([itself, chosen], axis=2).astype(jnp.int32)


def draw_counts(key, part):
    first_key, second_key, third_key = jax.random.split(key, 3)
    base = jax.random.randint(first_key, (MICRO, REGIONS), H_DEV // 4, H_DEV + 1)
    full_region = jax.random.randint(second_key, (MICRO, 1), 0, REGIONS)
    low_region = (full_region + 1 + jax.random.randint(third_key, (MICRO, 1), 0, REGIONS - 1)) % REGIONS
    region_ids = jnp.arange(REGIONS)[None, :]
    base = jnp.where(region_ids == full_region, H_DEV, jnp.where(region_ids == low_region, H_DEV // 4, base))
    return base.astype(jnp.int32)


def draw_w_qkv(key, part):
    first_key = jax.random.fold_in(key, 0)
    values = jax.random.normal(first_key, (BLOCKS, D, 3 * D), jnp.float32) * D ** (-0.5)
    return values.astype(jnp.bfloat16)


def shard_levels(key, extent, pieces, low, top_value):
    def one(dim, blocks):
        heights = jax.random.uniform(jax.random.fold_in(jax.random.fold_in(key, 6), dim), (blocks,), jnp.float32, low / len(pieces), top_value / len(pieces))
        return jnp.repeat(jnp.exp(heights), extent[dim] // blocks).reshape((-1,) + (1,) * (len(extent) - dim - 1))

    gain = one(*pieces[0])
    for cut in pieces[1:]:
        gain = gain * one(*cut)
    return gain


def gaussian(key, dims, width, bound, cuts=(), held_as=jnp.bfloat16):
    entries = width * jax.random.normal(key, dims, jnp.float32)
    if cuts:
        entries = entries * shard_levels(key, dims, cuts, -0.22, 0.18)
    return jnp.clip(entries, -bound, bound).astype(held_as)


def setup_inputs(seed: int = 0) -> dict:
    arg_keys = jax.random.split(jax.random.key(seed), 9)
    hits = gaussian(arg_keys[0], (MICRO, HITS, D), 1.0, 6.0, ((0, 2), (1, 256)))
    order = jax.vmap(lambda own: jax.random.permutation(own, H_DEV))(jax.random.split(arg_keys[1], MICRO * REGIONS)).reshape((MICRO, REGIONS, H_DEV)).astype(jnp.int32)
    links = draw_links(jax.random.fold_in(arg_keys[8], 71), 0)
    counts = draw_counts(jax.random.fold_in(arg_keys[8], 71), 0)
    w_qkv = draw_w_qkv(jax.random.fold_in(arg_keys[8], 71), 0)
    w_out = gaussian(arg_keys[5], (BLOCKS, D, D), D ** -0.5, 0.25, ((0, 2),))
    w_up = gaussian(arg_keys[6], (BLOCKS, D, FF), D ** -0.5, 0.25, ((0, 2),))
    w_down = gaussian(arg_keys[7], (BLOCKS, FF, D), FF ** -0.5, 0.125, ((0, 2),))
    return {"hits": hits, "order": order, "links": links, "counts": counts, "w_qkv": w_qkv, "w_out": w_out, "w_up": w_up, "w_down": w_down}


epsilon = 1e-05

def normalize(state):
    values = state.astype(jnp.float32)
    center = lax.optimization_barrier(jnp.mean(values, axis=-1, keepdims=True))
    spread = lax.optimization_barrier(jnp.mean((values - center) ** 2, axis=-1, keepdims=True))
    return ((values - center) * lax.rsqrt(spread + epsilon)).astype(jnp.bfloat16)

def attend(queries, padded_keys, padded_values, padded_valid, index):
    patch_count = index.shape[0]
    links_count = index.shape[1]
    query_part = queries.reshape(patch_count, PATCH, HEADS, HEAD_DIM).astype(jnp.float32)
    key_part = padded_keys.reshape(-1, PATCH, HEADS, HEAD_DIM)[index]
    key_part = key_part.reshape(patch_count, links_count * PATCH, HEADS, HEAD_DIM).astype(jnp.float32)
    value_part = padded_values.reshape(-1, PATCH, HEADS, HEAD_DIM)[index]
    value_part = value_part.reshape(patch_count, links_count * PATCH, HEADS, HEAD_DIM).astype(jnp.float32)
    key_mask = padded_valid.reshape(-1, PATCH)[index].reshape(patch_count, links_count * PATCH)
    scores = jnp.einsum('pqhd,pkhd->phqk', query_part, key_part) * HEAD_DIM ** (-0.5)
    scores = jnp.where(key_mask[:, None, None, :], scores, -1e+30)
    highest = lax.optimization_barrier(jnp.max(scores, axis=-1, keepdims=True))
    weights = jnp.exp(scores - highest)
    probs = (weights / lax.optimization_barrier(jnp.sum(weights, axis=-1, keepdims=True))).astype(jnp.bfloat16)
    output = jnp.einsum('phqk,pkhd->pqhd', probs.astype(jnp.float32), value_part)
    return output.reshape(patch_count * PATCH, D).astype(jnp.bfloat16)

def run_block(state, index, padded_valid, weight_qkv, weight_out, weight_up, weight_down):
    normed = normalize(state)
    mixed = jnp.dot(normed, weight_qkv, preferred_element_type=jnp.float32).astype(jnp.bfloat16)
    queries = mixed[:, :D]
    margin = REACH * PATCH
    padded_keys = jnp.pad(mixed[:, D:2 * D], ((margin, margin), (0, 0)))
    padded_values = jnp.pad(mixed[:, 2 * D:], ((margin, margin), (0, 0)))
    attended = attend(queries, padded_keys, padded_values, padded_valid, index)
    middle = (state.astype(jnp.float32) + jnp.dot(attended, weight_out, preferred_element_type=jnp.float32)).astype(jnp.bfloat16)
    normed_mlp = normalize(middle)
    hidden = jax.nn.gelu(jnp.dot(normed_mlp, weight_up, preferred_element_type=jnp.float32), approximate=False).astype(jnp.bfloat16)
    return (middle.astype(jnp.float32) + jnp.dot(hidden, weight_down, preferred_element_type=jnp.float32)).astype(jnp.bfloat16)

def reference(hits, order, links, counts, w_qkv, w_out, w_up, w_down):

    def one_event(event_index):
        regional = hits[event_index].reshape(REGIONS, H_DEV, D)
        ordered = regional[jnp.arange(REGIONS)[:, None], order[event_index]].reshape(HITS, D)
        position = jnp.arange(HITS)
        valid = position % H_DEV < counts[event_index][position // H_DEV]
        margin = REACH * PATCH
        padded_valid = jnp.pad(valid, (margin, margin))
        index = (links[event_index] + REACH).astype(jnp.int32)
        state = ordered
        for block_index in range(BLOCKS):
            state = run_block(state, index, padded_valid, w_qkv[block_index], w_out[block_index], w_up[block_index], w_down[block_index])
        return jnp.where(valid[:, None], state, jnp.zeros_like(state))
    return lax.map(one_event, jnp.arange(MICRO))
```

```python
import functools

import jax
import jax.numpy as jnp
from jax import lax
from jax.experimental import pallas as pl
from jax.experimental.pallas import tpu as pltpu
from jax.sharding import PartitionSpec as P

HEADS = 8
HEAD = 64
D = 512
PATCH = 128
LINKS = 3
PAIRS = HEADS // 2
EPS = 1e-05
BF16 = jnp.bfloat16
F32 = jnp.float32

QKV, OUT, UP, DOWN, SLOTS = 0, 3, 4, 8, 12


def dot(a, b):
    return jnp.dot(a, b, preferred_element_type=F32)


def normalize(values):
    center = jnp.mean(values, axis=-1, keepdims=True)
    shifted = values - center
    spread = jnp.mean(shifted * shifted, axis=-1, keepdims=True)
    return (shifted * lax.rsqrt(spread + EPS)).astype(BF16)


def gelu(x):
    return 0.5 * x * (1.0 + lax.erf(x * (0.5**0.5)))


def arrange_kernel(
    hits_hbm, order_hbm, w_qkv, w_out, w_up, w_down, ordered, packed, hits, order, sem
):
    event = lax.axis_index("section")
    pairs = [(hits_hbm.at[0], hits), (order_hbm.at[event], order)]
    for i in range(3):
        pairs.append((w_qkv.at[0, :, pl.ds(i * D, D)], packed.at[QKV + i]))
    pairs.append((w_out.at[0], packed.at[OUT]))
    for i in range(4):
        pairs.append((w_up.at[0, :, pl.ds(i * D, D)], packed.at[UP + i]))
    for i in range(4):
        pairs.append((w_down.at[0, pl.ds(i * D, D), :], packed.at[DOWN + i]))
    copies = [pltpu.make_async_copy(a, b, sem.at[i]) for i, (a, b) in enumerate(pairs)]
    for copy in copies:
        copy.start()
    copies[0].wait()
    copies[1].wait()
    rows = hits.shape[0]
    source_row = lax.broadcasted_iota(jnp.int32, (rows, rows), 0)
    chosen = jnp.where(source_row == order[...], 1.0, 0.0).T.astype(BF16)
    ordered[...] = dot(chosen, hits[...]).astype(BF16)
    for copy in copies[2:]:
        copy.wait()


def arrange(hits, order, *weights):
    rows = hits.shape[1]
    vmem = pl.BlockSpec(memory_space=pltpu.VMEM)
    args = [pltpu.with_memory_space_constraint(a, pltpu.HBM) for a in (hits, order, *weights)]
    return pl.pallas_call(
        arrange_kernel,
        name="arrange",
        out_shape=(
            jax.ShapeDtypeStruct((rows, D), BF16),
            jax.ShapeDtypeStruct((SLOTS, D, D), BF16),
        ),
        in_specs=[pl.BlockSpec(memory_space=pltpu.HBM)] * 6,
        out_specs=(vmem, vmem),
        scratch_shapes=[
            pltpu.VMEM((rows, D), BF16),
            pltpu.VMEM((1, rows), jnp.int32),
            pltpu.SemaphoreType.DMA((SLOTS + 2,)),
        ],
        compiler_params=pltpu.CompilerParams(vmem_limit_bytes=20 << 20),
        cost_estimate=pl.CostEstimate(
            flops=2 * rows * rows * D, bytes_accessed=13 << 20, transcendentals=0
        ),
    )(*args)


def fetch(block, own, came, weights, sem, slots):
    section = lax.axis_index("section")

    def copies(source):
        return [
            pltpu.make_async_copy(source.at[slot], weights.at[at], sem.at[at])
            for at, slot in enumerate(slots)
        ]

    @pl.when(section == block)
    def _():
        for copy in copies(own):
            copy.start()

    @pl.when(section != block)
    def _():
        for copy in copies(came):
            copy.start()

    waits = dict(zip(slots, copies(own)))
    place = {slot: at for at, slot in enumerate(slots)}

    def weight(slot):
        if waits[slot] is not None:
            waits[slot].wait()
            waits[slot] = None
        return weights[place[slot]]

    return weight


def project_kernel(block, state, own, came, mixed, weights, sem):
    weight = fetch(block, own, came, weights, sem, (QKV, QKV + 1, QKV + 2))
    normed = normalize(state[...].astype(F32))
    for i in range(3):
        part = dot(normed, weight(QKV + i)).astype(BF16)
        if i == 0:
            part = part * jnp.asarray(HEAD**-0.5, BF16)
        mixed[:, i * D : (i + 1) * D] = part


def project(block, state, own, came):
    rows = state.shape[0]
    any_space = pl.BlockSpec(memory_space=pl.ANY)
    vmem = pl.BlockSpec(memory_space=pltpu.VMEM)
    return pl.pallas_call(
        functools.partial(project_kernel, block),
        name=f"project_{block}",
        out_shape=jax.ShapeDtypeStruct((rows, 3 * D), BF16),
        in_specs=[vmem, any_space, any_space],
        out_specs=vmem,
        scratch_shapes=[pltpu.VMEM((3, D, D), BF16), pltpu.SemaphoreType.DMA((3,))],
        compiler_params=pltpu.CompilerParams(vmem_limit_bytes=10 << 20),
        cost_estimate=pl.CostEstimate(
            flops=6 * rows * D * D, bytes_accessed=3 << 20, transcendentals=0
        ),
    )(state, own, came)


def block_kernel(
    block,
    last,
    links,
    counts,
    state,
    mixed,
    near_a,
    near_b,
    own,
    came,
    result,
    weights,
    keys,
    values,
    attended,
    sem,
):
    weight = fetch(block, own, came, weights, sem, tuple(range(QKV + 1, SLOTS)))
    event = lax.axis_index("section")
    region = lax.axis_index("region")
    regions = counts.shape[1]
    rows = state.shape[0]
    patches = rows // PATCH
    even = lax.rem(region, 2) == 0
    region_a = jnp.where(even, region + 1, region - 1)
    region_b = jnp.where(even, region - 1, region + 1)
    lane = lax.broadcasted_iota(jnp.int32, (1, 2 * HEAD), 1)
    low = lane < HEAD
    ones_low = jnp.broadcast_to(jnp.where(low, 1.0, 0.0).astype(BF16), (PATCH, PATCH))
    ones_high = jnp.broadcast_to(jnp.where(low, 0.0, 1.0).astype(BF16), (PATCH, PATCH))

    def spread(slot, key_rows, value_rows):
        for pair in range(PAIRS):
            k = key_rows[:, pair * 128 : (pair + 1) * 128]
            v = value_rows[:, pair * 128 : (pair + 1) * 128]
            keys[slot, pair, 0:PATCH, :] = k * ones_low
            keys[slot, pair, PATCH : 2 * PATCH, :] = k * ones_high
            values[slot, pair, 0:PATCH, 0:128] = v * ones_low
            values[slot, pair, PATCH : 2 * PATCH, 0:128] = v * ones_high
            values[slot, pair, 0:PATCH, 128:256] = ones_low
            values[slot, pair, PATCH : 2 * PATCH, 128:256] = ones_high

    for patch in range(patches):
        here = pl.ds(patch * PATCH, PATCH)
        spread(patch, mixed[here, D : 2 * D], mixed[here, 2 * D : 3 * D])
    for base, near in ((patches, near_a), (2 * patches, near_b)):
        normed = normalize(near[...].astype(F32))
        key_rows = dot(normed, weight(QKV + 1)).astype(BF16)
        value_rows = dot(normed, weight(QKV + 2)).astype(BF16)
        for patch in range(patches):
            cut = slice(patch * PATCH, (patch + 1) * PATCH)
            spread(base + patch, key_rows[cut], value_rows[cut])

    count_own = counts[event, region]
    count_a = counts[event, jnp.clip(region_a, 0, regions - 1)]
    count_b = counts[event, jnp.clip(region_b, 0, regions - 1)]
    key_lane = jnp.bitwise_and(lax.broadcasted_iota(jnp.int32, (PATCH, 2 * PATCH), 1), PATCH - 1)
    for patch in range(patches):
        slots, valid = [], []
        for link in range(LINKS):
            linked = links[event, patch, link]
            owner = lax.div(linked, patches)
            half = lax.rem(linked, patches)
            base = jnp.where(owner == region, 0, jnp.where(owner == region_a, 1, 2))
            count = jnp.where(base == 0, count_own, jnp.where(base == 1, count_a, count_b))
            slots.append(base * patches + half)
            valid.append(key_lane < count - half * PATCH)
        here = pl.ds(patch * PATCH, PATCH)
        for pair in range(PAIRS):
            across = pl.ds(pair * 128, 128)
            query = mixed[here, across]
            scores = [
                jnp.where(
                    valid[link],
                    lax.dot_general(
                        query,
                        keys[slots[link], pair],
                        (((1,), (1,)), ((), ())),
                        preferred_element_type=F32,
                    ),
                    -1e30,
                )
                for link in range(LINKS)
            ]
            top = functools.reduce(jnp.maximum, scores)
            top_low = jnp.max(top[:, :PATCH], axis=-1, keepdims=True)
            top_high = jnp.max(top[:, PATCH:], axis=-1, keepdims=True)
            total = None
            for link in range(LINKS):
                weighed = jnp.concatenate(
                    [
                        jnp.exp(scores[link][:, :PATCH] - top_low),
                        jnp.exp(scores[link][:, PATCH:] - top_high),
                    ],
                    axis=1,
                ).astype(BF16)
                part = dot(weighed, values[slots[link], pair])
                total = part if total is None else total + part
            attended[here, across] = (total[:, :128] / total[:, 128:]).astype(BF16)

    middle = (state[...].astype(F32) + dot(attended[...], weight(OUT))).astype(BF16)
    middle = middle.astype(F32)
    normed = normalize(middle)
    total = middle
    for part in range(4):
        hidden = gelu(dot(normed, weight(UP + part))).astype(BF16)
        total = total + dot(hidden, weight(DOWN + part))
    total = total.astype(BF16)
    if last:
        row = lax.broadcasted_iota(jnp.int32, (rows, D), 0)
        total = jnp.where(row < count_own, total.astype(F32), 0.0).astype(BF16)
    result[...] = total


def run_block(block, last, links, counts, state, mixed, near_a, near_b, own, came):
    rows = state.shape[0]
    patches = rows // PATCH
    any_space = pl.BlockSpec(memory_space=pl.ANY)
    vmem = pl.BlockSpec(memory_space=pltpu.VMEM)
    smem = pl.BlockSpec(memory_space=pltpu.SMEM)
    return pl.pallas_call(
        functools.partial(block_kernel, block, last),
        name=f"block_{block}",
        out_shape=jax.ShapeDtypeStruct((rows, D), BF16),
        in_specs=[smem, smem, vmem, vmem, vmem, vmem, any_space, any_space],
        out_specs=vmem,
        scratch_shapes=[
            pltpu.VMEM((SLOTS - 1, D, D), BF16),
            pltpu.VMEM((3 * patches, PAIRS, 2 * PATCH, 128), BF16),
            pltpu.VMEM((3 * patches, PAIRS, 2 * PATCH, 256), BF16),
            pltpu.VMEM((rows, D), BF16),
            pltpu.SemaphoreType.DMA((SLOTS - 1,)),
        ],
        compiler_params=pltpu.CompilerParams(vmem_limit_bytes=32 << 20),
        cost_estimate=pl.CostEstimate(
            flops=4 * 10**9, bytes_accessed=8 << 20, transcendentals=2 * 10**6
        ),
    )(links, counts, state, mixed, near_a, near_b, own, came)


def per_device(hits, order, links, counts, w_qkv, w_out, w_up, w_down):
    regions = counts.shape[1]
    pairs_a = [(i, i ^ 1) for i in range(regions)]
    pairs_b = []
    for i in range(1, regions - 1, 2):
        pairs_b += [(i, i + 1), (i + 1, i)]
    ordered, own = arrange(hits, order, w_qkv, w_out, w_up, w_down)
    came = lax.ppermute(own, "section", [(0, 1), (1, 0)])
    state = ordered
    for block in range(2):
        near_b = lax.ppermute(state, "region", pairs_b)
        near_a = lax.ppermute(state, "region", pairs_a)
        mixed = project(block, state, own, came)
        state = run_block(
            block, block == 1, links, counts, state, mixed, near_a, near_b, own, came
        )
    return state[None]


def solution(mesh):
    in_specs = (
        P("section", "region", None),
        P(None, "region", None),
        P(None, "region", None),
        P(),
        P("section", None, None),
        P("section", None, None),
        P("section", None, None),
        P("section", None, None),
    )
    out_specs = P("section", "region", None)
    return jax.shard_map(
        per_device, mesh=mesh, in_specs=in_specs, out_specs=out_specs, check_vma=False
    )
```

```python
import functools

import jax
import jax.numpy as jnp
from jax import lax
from jax.experimental import pallas as pl
from jax.experimental.pallas import tpu as pltpu
from jax.sharding import PartitionSpec as P


HEADS = 8
HEAD = 64
D = 512
PATCH = 128
LINKS = 3
PAIRS = HEADS // 2
EPS = 1e-05
FF = 2048
WIDTH = 1024
LIMIT = 16 << 20
BF16 = jnp.bfloat16
F32 = jnp.float32

QKV, OUT, FIRST = 0, 3, 4


def dot(a, b):
    return jnp.dot(a, b, preferred_element_type=F32)


def normalize(values):
    center = jnp.mean(values, axis=-1, keepdims=True)
    shifted = values - center
    spread = jnp.mean(shifted * shifted, axis=-1, keepdims=True)
    return (shifted * lax.rsqrt(spread + EPS)).astype(BF16)


def gelu(x):
    return 0.5 * x * (1.0 + lax.erf(x * (0.5**0.5)))


def copies_of(pairs, sem):
    return [pltpu.make_async_copy(a, b, sem.at[i]) for i, (a, b) in enumerate(pairs)]


def arrange_kernel(hits_hbm, order_hbm, w_qkv, w_out, ordered, packed, hits, order, sem):
    event = lax.axis_index("section")
    pairs = [(hits_hbm.at[0], hits), (order_hbm.at[event], order)]
    for i in range(3):
        pairs.append((w_qkv.at[0, :, pl.ds(i * D, D)], packed.at[QKV + i]))
    pairs.append((w_out.at[0], packed.at[OUT]))
    copies = copies_of(pairs, sem)
    for copy in copies:
        copy.start()
    copies[0].wait()
    copies[1].wait()
    rows = hits.shape[0]
    source_row = lax.broadcasted_iota(jnp.int32, (rows, rows), 0)
    chosen = jnp.where(source_row == order[...], 1.0, 0.0).T.astype(BF16)
    ordered[...] = dot(chosen, hits[...]).astype(BF16)
    for copy in copies[2:]:
        copy.wait()


def arrange(hits, order, w_qkv, w_out):
    rows = hits.shape[1]
    vmem = pl.BlockSpec(memory_space=pltpu.VMEM)
    args = [pltpu.with_memory_space_constraint(a, pltpu.HBM) for a in (hits, order, w_qkv, w_out)]
    return pl.pallas_call(
        arrange_kernel,
        name="arrange",
        out_shape=(
            jax.ShapeDtypeStruct((rows, D), BF16),
            jax.ShapeDtypeStruct((FIRST, D, D), BF16),
        ),
        in_specs=[pl.BlockSpec(memory_space=pltpu.HBM)] * 4,
        out_specs=(vmem, vmem),
        scratch_shapes=[
            pltpu.VMEM((rows, D), BF16),
            pltpu.VMEM((1, rows), jnp.int32),
            pltpu.SemaphoreType.DMA((FIRST + 2,)),
        ],
        compiler_params=pltpu.CompilerParams(vmem_limit_bytes=20 << 20),
        cost_estimate=pl.CostEstimate(
            flops=2 * rows * rows * D, bytes_accessed=4 << 20, transcendentals=0
        ),
    )(*args)


def with_weights(block, own, came, body):
    section = lax.axis_index("section")

    @pl.when(section == block)
    def _():
        body(*own)

    @pl.when(section != block)
    def _():
        body(*came)


def prepare_kernel(block, state, own, came, queries, mixed):
    low = lax.broadcasted_iota(jnp.int32, (PATCH, 128), 1) < HEAD
    scale = jnp.asarray(HEAD**-0.5, BF16)
    low_scale = jnp.where(low, scale, 0.0).astype(BF16)
    high_scale = jnp.where(low, 0.0, scale).astype(BF16)

    def body(weights):
        normed = normalize(state[...].astype(F32))
        query = dot(normed, weights[QKV]).astype(BF16)
        for patch in range(state.shape[0] // PATCH):
            for pair in range(PAIRS):
                part = query[patch * PATCH : (patch + 1) * PATCH, pair * 128 : (pair + 1) * 128]
                queries[patch, pair, 0:PATCH, :] = part * low_scale
                queries[patch, pair, PATCH : 2 * PATCH, :] = part * high_scale
        mixed[:, 0:D] = dot(normed, weights[QKV + 1]).astype(BF16)
        mixed[:, D : 2 * D] = dot(normed, weights[QKV + 2]).astype(BF16)

    with_weights(block, (own,), (came,), body)


def prepare(block, state, own, came):
    rows = state.shape[0]
    vmem = pl.BlockSpec(memory_space=pltpu.VMEM)
    return pl.pallas_call(
        functools.partial(prepare_kernel, block),
        out_shape=(
            jax.ShapeDtypeStruct((rows // PATCH, PAIRS, 2 * PATCH, 128), BF16),
            jax.ShapeDtypeStruct((rows, 2 * D), BF16),
        ),
        in_specs=[vmem] * 3,
        out_specs=(vmem, vmem),
        compiler_params=pltpu.CompilerParams(vmem_limit_bytes=LIMIT),
        cost_estimate=pl.CostEstimate(
            flops=6 * rows * D * D, bytes_accessed=4 << 20, transcendentals=0
        ),
    )(state, own, came)


def attend_kernel(
    block,
    links,
    counts,
    state,
    queries,
    mixed,
    near_a,
    near_b,
    own,
    came,
    middle,
    near,
    attended,
    sem,
):
    event = lax.axis_index("section")
    region = lax.axis_index("region")
    regions = counts.shape[1]
    rows = state.shape[0]
    patches = rows // PATCH
    bring = pltpu.make_async_copy(mixed, near.at[pl.ds(0, rows)], sem)
    bring.start()
    even = lax.rem(region, 2) == 0
    region_a = jnp.where(even, region + 1, region - 1)
    region_b = jnp.where(even, region - 1, region + 1)
    count_own = counts[event, region]
    count_a = counts[event, jnp.clip(region_a, 0, regions - 1)]
    count_b = counts[event, jnp.clip(region_b, 0, regions - 1)]
    key_lane = lax.broadcasted_iota(jnp.int32, (2 * PATCH, PATCH), 1)
    low = lax.broadcasted_iota(jnp.int32, (PATCH, 128), 1) < HEAD
    ones = jnp.ones((PATCH, 128), BF16)

    def body(weights):
        for i, other in enumerate((near_a, near_b)):
            normed = normalize(other[...].astype(F32))
            here = slice((i + 1) * rows, (i + 2) * rows)
            near[here, 0:D] = dot(normed, weights[QKV + 1]).astype(BF16)
            near[here, D : 2 * D] = dot(normed, weights[QKV + 2]).astype(BF16)
        bring.wait()
        for patch in range(patches):
            places, valid = [], []
            for link in range(LINKS):
                linked = links[event, patch, link]
                owner = lax.div(linked, patches)
                half = lax.rem(linked, patches)
                base = jnp.where(owner == region, 0, jnp.where(owner == region_a, 1, 2))
                count = jnp.where(base == 0, count_own, jnp.where(base == 1, count_a, count_b))
                places.append(pl.multiple_of((base * patches + half) * PATCH, PATCH))
                valid.append(key_lane < count - half * PATCH)
            for pair in range(PAIRS):
                across = slice(pair * 128, (pair + 1) * 128)
                query = queries[patch, pair]
                scores = []
                for link in range(LINKS):
                    score = lax.dot_general(
                        query,
                        near[pl.ds(places[link], PATCH), across],
                        (((1,), (1,)), ((), ())),
                        preferred_element_type=F32,
                    )
                    scores.append(jnp.where(valid[link], score, -1e30))
                top = jnp.max(functools.reduce(jnp.maximum, scores), axis=-1, keepdims=True)
                total = None
                for link in range(LINKS):
                    weighed = jnp.exp(scores[link] - top).astype(BF16)
                    value = near[pl.ds(places[link], PATCH), D + pair * 128 : D + (pair + 1) * 128]
                    part = dot(weighed, jnp.concatenate([value, ones], axis=1))
                    total = part if total is None else total + part
                summed = jnp.where(low, total[:PATCH, :128], total[PATCH:, :128])
                mass = jnp.where(low, total[:PATCH, 128:], total[PATCH:, 128:])
                attended[patch * PATCH : (patch + 1) * PATCH, across] = (summed / mass).astype(BF16)
        middle[...] = (state[...].astype(F32) + dot(attended[...], weights[OUT])).astype(BF16)

    with_weights(block, (own,), (came,), body)


def attend(block, links, counts, state, queries, mixed, near_a, near_b, own, came):
    rows = state.shape[0]
    vmem = pl.BlockSpec(memory_space=pltpu.VMEM)
    smem = pl.BlockSpec(memory_space=pltpu.SMEM)
    return pl.pallas_call(
        functools.partial(attend_kernel, block),
        out_shape=jax.ShapeDtypeStruct((rows, D), BF16),
        in_specs=[smem, smem] + [vmem] * 7,
        out_specs=vmem,
        scratch_shapes=[
            pltpu.VMEM((3 * rows, 2 * D), BF16),
            pltpu.VMEM((rows, D), BF16),
            pltpu.SemaphoreType.DMA,
        ],
        compiler_params=pltpu.CompilerParams(vmem_limit_bytes=LIMIT),
        cost_estimate=pl.CostEstimate(
            flops=10**9, bytes_accessed=4 << 20, transcendentals=8 * 10**5
        ),
    )(links, counts, state, queries, mixed, near_a, near_b, own, came)


def feed_kernel(block, last, counts, middle_ref, up_own, down_own, up_came, down_came, result):
    def body(up, down):
        middle = middle_ref[...].astype(F32)
        normed = normalize(middle)
        total = middle
        for part in range(0, FF, WIDTH):
            hidden = gelu(dot(normed, up[0, :, part : part + WIDTH])).astype(BF16)
            total = total + dot(hidden, down[0, part : part + WIDTH, :])
        total = total.astype(BF16)
        if last:
            count = counts[lax.axis_index("section"), lax.axis_index("region")]
            row = lax.broadcasted_iota(jnp.int32, total.shape, 0)
            total = jnp.where(row < count, total.astype(F32), 0.0).astype(BF16)
        result[...] = total

    with_weights(block, (up_own, down_own), (up_came, down_came), body)


def feed(block, last, counts, middle, *weights):
    rows = middle.shape[0]
    vmem = pl.BlockSpec(memory_space=pltpu.VMEM)
    smem = pl.BlockSpec(memory_space=pltpu.SMEM)
    return pl.pallas_call(
        functools.partial(feed_kernel, block, last),
        out_shape=jax.ShapeDtypeStruct((rows, D), BF16),
        in_specs=[smem] + [vmem] * 5,
        out_specs=vmem,
        compiler_params=pltpu.CompilerParams(vmem_limit_bytes=LIMIT),
        cost_estimate=pl.CostEstimate(
            flops=4 * rows * FF * D, bytes_accessed=5 << 20, transcendentals=10**6
        ),
    )(counts, middle, *weights)


def per_device(hits, order, links, counts, w_qkv, w_out, w_up, w_down):
    regions = counts.shape[1]
    pairs_a = [(i, i ^ 1) for i in range(regions)]
    pairs_b = []
    for i in range(1, regions - 1, 2):
        pairs_b += [(i, i + 1), (i + 1, i)]
    swap = [(0, 1), (1, 0)]
    ordered, own = arrange(hits, order, w_qkv, w_out)
    state = ordered
    for block in range(2):
        near_b = lax.ppermute(state, "region", pairs_b)
        if block == 0:
            came = lax.ppermute(own, "section", swap)
        near_a = lax.ppermute(state, "region", pairs_a)
        if block == 0:
            up_came = lax.ppermute(w_up, "section", swap)
            down_came = lax.ppermute(w_down, "section", swap)
            second = (w_up, w_down, up_came, down_came)
        queries, mixed = prepare(block, state, own, came)
        middle = attend(block, links, counts, state, queries, mixed, near_a, near_b, own, came)
        state = feed(block, block == 1, counts, middle, *second)
    return state[None]


def solution(mesh):
    in_specs = (
        P("section", "region", None),
        P(None, "region", None),
        P(None, "region", None),
        P(),
        P("section", None, None),
        P("section", None, None),
        P("section", None, None),
        P("section", None, None),
    )
    out_specs = P("section", "region", None)
    return jax.shard_map(
        per_device, mesh=mesh, in_specs=in_specs, out_specs=out_specs, check_vma=False
    )
```

```python
import functools

import jax
import jax.numpy as jnp
from jax import lax
from jax.experimental import pallas as pl
from jax.experimental.pallas import tpu as pltpu
from jax.sharding import PartitionSpec as P


HEADS = 8
HEAD = 64
D = 512
PATCH = 128
LINKS = 3
PAIRS = HEADS // 2
EPS = 1e-05
FF = 2048
WIDTH = 1024
LIMIT = 16 << 20
BF16 = jnp.bfloat16
F32 = jnp.float32

QKV, OUT, FIRST = 0, 3, 4


def dot(a, b):
    return jnp.dot(a, b, preferred_element_type=F32)


def normalize(values):
    center = jnp.mean(values, axis=-1, keepdims=True)
    shifted = values - center
    spread = jnp.mean(shifted * shifted, axis=-1, keepdims=True)
    return (shifted * lax.rsqrt(spread + EPS)).astype(BF16)


def gelu(x):
    return 0.5 * x * (1.0 + lax.erf(x * (0.5**0.5)))


def copies_of(pairs, sem):
    return [pltpu.make_async_copy(a, b, sem.at[i]) for i, (a, b) in enumerate(pairs)]


def arrange_kernel(hits_hbm, order_hbm, w_qkv, w_out, ordered, sent, packed, hits, order, sem):
    event = lax.axis_index("section")
    pairs = [(hits_hbm.at[0], hits), (order_hbm.at[event], order)]
    for i in range(3):
        pairs.append((w_qkv.at[0, :, pl.ds(i * D, D)], packed.at[QKV + i]))
    pairs.append((w_out.at[0], packed.at[OUT]))
    copies = copies_of(pairs, sem)
    for copy in copies:
        copy.start()
    copies[0].wait()
    copies[1].wait()
    rows = hits.shape[0]
    source_row = lax.broadcasted_iota(jnp.int32, (rows, rows), 0)
    chosen = jnp.where(source_row == order[...], 1.0, 0.0).T.astype(BF16)
    state = dot(chosen, hits[...]).astype(BF16)
    ordered[...] = state
    sent[...] = normalize(state.astype(F32))
    for copy in copies[2:]:
        copy.wait()


def arrange(hits, order, w_qkv, w_out):
    rows = hits.shape[1]
    vmem = pl.BlockSpec(memory_space=pltpu.VMEM)
    args = [pltpu.with_memory_space_constraint(a, pltpu.HBM) for a in (hits, order, w_qkv, w_out)]
    return pl.pallas_call(
        arrange_kernel,
        name="arrange",
        out_shape=(
            jax.ShapeDtypeStruct((rows, D), BF16),
            jax.ShapeDtypeStruct((rows, D), BF16),
            jax.ShapeDtypeStruct((FIRST, D, D), BF16),
        ),
        in_specs=[pl.BlockSpec(memory_space=pltpu.HBM)] * 4,
        out_specs=(vmem,) * 3,
        scratch_shapes=[
            pltpu.VMEM((rows, D), BF16),
            pltpu.VMEM((1, rows), jnp.int32),
            pltpu.SemaphoreType.DMA((FIRST + 2,)),
        ],
        compiler_params=pltpu.CompilerParams(vmem_limit_bytes=20 << 20),
        cost_estimate=pl.CostEstimate(
            flops=2 * rows * rows * D, bytes_accessed=4 << 20, transcendentals=0
        ),
    )(*args)


def with_weights(block, own, came, body):
    section = lax.axis_index("section")

    @pl.when(section == block)
    def _():
        body(*own)

    @pl.when(section != block)
    def _():
        body(*came)


def turned(values, patch, pair):
    part = values[patch * PATCH : (patch + 1) * PATCH, pair * 128 : (pair + 1) * 128]
    return part.T.astype(BF16)


def prepare_kernel(block, sent, own, came, queries, keys, values):
    low = lax.broadcasted_iota(jnp.int32, (PATCH, 128), 1) < HEAD
    scale = jnp.asarray(HEAD**-0.5, BF16)
    low_scale = jnp.where(low, scale, 0.0).astype(BF16)
    high_scale = jnp.where(low, 0.0, scale).astype(BF16)

    def body(weights):
        normed = sent[...]
        query = dot(normed, weights[QKV]).astype(BF16)
        keys[...] = dot(normed, weights[QKV + 1]).astype(BF16)
        value = dot(normed, weights[QKV + 2])
        for patch in range(sent.shape[0] // PATCH):
            for pair in range(PAIRS):
                part = query[patch * PATCH : (patch + 1) * PATCH, pair * 128 : (pair + 1) * 128]
                queries[patch, pair, 0:PATCH, :] = part * low_scale
                queries[patch, pair, PATCH : 2 * PATCH, :] = part * high_scale
                values[patch, pair] = turned(value, patch, pair)

    with_weights(block, (own,), (came,), body)


def prepare(block, sent, own, came):
    rows = sent.shape[0]
    patches = rows // PATCH
    vmem = pl.BlockSpec(memory_space=pltpu.VMEM)
    return pl.pallas_call(
        functools.partial(prepare_kernel, block),
        out_shape=(
            jax.ShapeDtypeStruct((patches, PAIRS, 2 * PATCH, 128), BF16),
            jax.ShapeDtypeStruct((rows, D), BF16),
            jax.ShapeDtypeStruct((patches, PAIRS, 128, PATCH), BF16),
        ),
        in_specs=[vmem] * 3,
        out_specs=(vmem,) * 3,
        compiler_params=pltpu.CompilerParams(vmem_limit_bytes=LIMIT),
        cost_estimate=pl.CostEstimate(
            flops=6 * rows * D * D, bytes_accessed=4 << 20, transcendentals=0
        ),
    )(sent, own, came)


def attend_kernel(
    block,
    links,
    counts,
    state,
    queries,
    own_keys,
    own_values,
    near_a,
    near_b,
    own,
    came,
    middle,
    keys,
    values,
    scores,
    tops,
    totals,
    attended,
    sem,
):
    event = lax.axis_index("section")
    region = lax.axis_index("region")
    regions = counts.shape[1]
    rows = state.shape[0]
    patches = rows // PATCH
    bring = copies_of(
        [(own_keys, keys.at[pl.ds(0, rows)]), (own_values, values.at[pl.ds(0, patches)])], sem
    )
    for copy in bring:
        copy.start()
    even = lax.rem(region, 2) == 0
    region_a = jnp.where(even, region + 1, region - 1)
    region_b = jnp.where(even, region - 1, region + 1)
    count_own = counts[event, region]
    count_a = counts[event, jnp.clip(region_a, 0, regions - 1)]
    count_b = counts[event, jnp.clip(region_b, 0, regions - 1)]
    key_row = lax.broadcasted_iota(jnp.int32, (PATCH, 2 * PATCH), 0)
    ones = jnp.ones((16, LINKS * PATCH), BF16)

    def body(weights):
        normed = jnp.concatenate([near_a[...], near_b[...]], axis=0)
        keys[rows : 3 * rows, :] = dot(normed, weights[QKV + 1]).astype(BF16)
        value = dot(normed, weights[QKV + 2])
        for patch in range(2 * patches):
            for pair in range(PAIRS):
                values[patches + patch, pair] = turned(value, patch, pair)
        for copy in bring:
            copy.wait()
        slots = []
        for patch in range(patches):
            valid = []
            for link in range(LINKS):
                linked = links[event, patch, link]
                owner = lax.div(linked, patches)
                half = lax.rem(linked, patches)
                base = jnp.where(owner == region, 0, jnp.where(owner == region_a, 1, 2))
                count = jnp.where(base == 0, count_own, jnp.where(base == 1, count_a, count_b))
                slots.append(base * patches + half)
                valid.append(key_row < count - half * PATCH)
            for pair in range(PAIRS):
                unit = patch * PAIRS + pair
                query = queries[patch, pair]
                top = None
                for link in range(LINKS):
                    start = pl.multiple_of(slots[patch * LINKS + link] * PATCH, PATCH)
                    score = lax.dot_general(
                        keys[pl.ds(start, PATCH), pair * 128 : (pair + 1) * 128],
                        query,
                        (((1,), (1,)), ((), ())),
                        preferred_element_type=F32,
                    )
                    score = jnp.where(valid[link], score, -1e30)
                    scores[unit, link * PATCH : (link + 1) * PATCH, :] = score
                    top = score if top is None else jnp.maximum(top, score)
                tops[unit] = jnp.broadcast_to(jnp.max(top, axis=0, keepdims=True), (8, 2 * PATCH))
        for patch in range(patches):
            for pair in range(PAIRS):
                unit = patch * PAIRS + pair
                weighed = jnp.exp(scores[unit] - tops[unit, 0:1, :]).astype(BF16)
                taken = jnp.concatenate(
                    [values[slot, pair] for slot in slots[patch * LINKS : (patch + 1) * LINKS]],
                    axis=1,
                )
                totals[unit] = dot(jnp.concatenate([taken, ones], axis=0), weighed)
        for patch in range(patches):
            for pair in range(PAIRS):
                unit = patch * PAIRS + pair
                share = 1.0 / totals[unit, 128:129, :]
                whole = jnp.concatenate(
                    [
                        totals[unit, 0:HEAD, 0:PATCH] * share[:, 0:PATCH],
                        totals[unit, HEAD:128, PATCH:] * share[:, PATCH:],
                    ],
                    axis=0,
                )
                attended[
                    patch * PATCH : (patch + 1) * PATCH, pair * 128 : (pair + 1) * 128
                ] = whole.T.astype(BF16)
        middle[...] = (state[...].astype(F32) + dot(attended[...], weights[OUT])).astype(BF16)

    with_weights(block, (own,), (came,), body)


def attend(block, links, counts, state, queries, keys, values, near_a, near_b, own, came):
    rows = state.shape[0]
    patches = rows // PATCH
    vmem = pl.BlockSpec(memory_space=pltpu.VMEM)
    smem = pl.BlockSpec(memory_space=pltpu.SMEM)
    return pl.pallas_call(
        functools.partial(attend_kernel, block),
        out_shape=jax.ShapeDtypeStruct((rows, D), BF16),
        in_specs=[smem, smem] + [vmem] * 8,
        out_specs=vmem,
        scratch_shapes=[
            pltpu.VMEM((3 * rows, D), BF16),
            pltpu.VMEM((3 * patches, PAIRS, 128, PATCH), BF16),
            pltpu.VMEM((patches * PAIRS, LINKS * PATCH, 2 * PATCH), F32),
            pltpu.VMEM((patches * PAIRS, 8, 2 * PATCH), F32),
            pltpu.VMEM((patches * PAIRS, 144, 2 * PATCH), F32),
            pltpu.VMEM((rows, D), BF16),
            pltpu.SemaphoreType.DMA((2,)),
        ],
        compiler_params=pltpu.CompilerParams(vmem_limit_bytes=LIMIT),
        cost_estimate=pl.CostEstimate(
            flops=10**9, bytes_accessed=4 << 20, transcendentals=8 * 10**5
        ),
    )(links, counts, state, queries, keys, values, near_a, near_b, own, came)


def feed_kernel(
    block, last, counts, middle_ref, up_own, down_own, up_came, down_came, result, *sent
):
    def body(up, down):
        middle = middle_ref[...].astype(F32)
        normed = normalize(middle)
        total = middle
        for part in range(0, FF, WIDTH):
            hidden = gelu(dot(normed, up[0, :, part : part + WIDTH])).astype(BF16)
            total = total + dot(hidden, down[0, part : part + WIDTH, :])
        total = total.astype(BF16)
        if last:
            count = counts[lax.axis_index("section"), lax.axis_index("region")]
            row = lax.broadcasted_iota(jnp.int32, total.shape, 0)
            total = jnp.where(row < count, total.astype(F32), 0.0).astype(BF16)
        else:
            sent[0][...] = normalize(total.astype(F32))
        result[...] = total

    with_weights(block, (up_own, down_own), (up_came, down_came), body)


def feed(block, last, counts, middle, *weights):
    rows = middle.shape[0]
    outputs = 1 if last else 2
    vmem = pl.BlockSpec(memory_space=pltpu.VMEM)
    smem = pl.BlockSpec(memory_space=pltpu.SMEM)
    return pl.pallas_call(
        functools.partial(feed_kernel, block, last),
        out_shape=(jax.ShapeDtypeStruct((rows, D), BF16),) * outputs,
        in_specs=[smem] + [vmem] * 5,
        out_specs=(vmem,) * outputs,
        compiler_params=pltpu.CompilerParams(vmem_limit_bytes=LIMIT),
        cost_estimate=pl.CostEstimate(
            flops=4 * rows * FF * D, bytes_accessed=5 << 20, transcendentals=10**6
        ),
    )(counts, middle, *weights)


def per_device(hits, order, links, counts, w_qkv, w_out, w_up, w_down):
    regions = counts.shape[1]
    pairs_a = [(i, i ^ 1) for i in range(regions)]
    pairs_b = []
    for i in range(1, regions - 1, 2):
        pairs_b += [(i, i + 1), (i + 1, i)]
    swap = [(0, 1), (1, 0)]
    state, sent, own = arrange(hits, order, w_qkv, w_out)
    for block in range(2):
        near_b = lax.ppermute(sent, "region", pairs_b)
        if block == 0:
            came = lax.ppermute(own, "section", swap)
        near_a = lax.ppermute(sent, "region", pairs_a)
        if block == 0:
            up_came = lax.ppermute(w_up, "section", swap)
            down_came = lax.ppermute(w_down, "section", swap)
            second = (w_up, w_down, up_came, down_came)
        queries, keys, values = prepare(block, sent, own, came)
        middle = attend(
            block,
            links,
            counts,
            state,
            queries,
            keys,
            values,
            near_a,
            near_b,
            own,
            came,
        )
        state, *sent = feed(block, block == 1, counts, middle, *second)
        sent = sent[0] if sent else None
    return state[None]


def solution(mesh):
    in_specs = (
        P("section", "region", None),
        P(None, "region", None),
        P(None, "region", None),
        P(),
        P("section", None, None),
        P("section", None, None),
        P("section", None, None),
        P("section", None, None),
    )
    out_specs = P("section", "region", None)
    return jax.shard_map(
        per_device, mesh=mesh, in_specs=in_specs, out_specs=out_specs, check_vma=False
    )
```

```python
import functools

import jax
import jax.numpy as jnp
from jax import lax
from jax.experimental import pallas as pl
from jax.experimental.pallas import tpu as pltpu
from jax.sharding import PartitionSpec as P


HEADS = 8
HEAD = 64
D = 512
PATCH = 128
LINKS = 3
PAIRS = HEADS // 2
EPS = 1e-05
FF = 2048
WIDTH = 1024
LIMIT = 16 << 20
BF16 = jnp.bfloat16
F32 = jnp.float32

QKV, OUT, FIRST = 0, 3, 4


def dot(a, b):
    return jnp.dot(a, b, preferred_element_type=F32)


def normalize(values):
    center = jnp.mean(values, axis=-1, keepdims=True)
    shifted = values - center
    spread = jnp.mean(shifted * shifted, axis=-1, keepdims=True)
    return (shifted * lax.rsqrt(spread + EPS)).astype(BF16)


def gelu(x):
    return 0.5 * x * (1.0 + lax.erf(x * (0.5**0.5)))


def copies_of(pairs, sem):
    return [pltpu.make_async_copy(a, b, sem.at[i]) for i, (a, b) in enumerate(pairs)]


def arrange_kernel(hits_hbm, order_hbm, w_qkv, w_out, ordered, sent, packed, hits, order, sem):
    event = lax.axis_index("section")
    pairs = [(hits_hbm.at[0], hits), (order_hbm.at[event], order)]
    for i in range(3):
        pairs.append((w_qkv.at[0, :, pl.ds(i * D, D)], packed.at[QKV + i]))
    pairs.append((w_out.at[0], packed.at[OUT]))
    copies = copies_of(pairs, sem)
    for copy in copies:
        copy.start()
    copies[0].wait()
    copies[1].wait()
    rows = hits.shape[0]
    source_row = lax.broadcasted_iota(jnp.int32, (rows, rows), 0)
    chosen = jnp.where(source_row == order[...], 1.0, 0.0).T.astype(BF16)
    state = dot(chosen, hits[...]).astype(BF16)
    ordered[...] = state
    sent[...] = normalize(state.astype(F32))
    for copy in copies[2:]:
        copy.wait()


def arrange(hits, order, w_qkv, w_out):
    rows = hits.shape[1]
    vmem = pl.BlockSpec(memory_space=pltpu.VMEM)
    args = [pltpu.with_memory_space_constraint(a, pltpu.HBM) for a in (hits, order, w_qkv, w_out)]
    return pl.pallas_call(
        arrange_kernel,
        name="arrange",
        out_shape=(
            jax.ShapeDtypeStruct((rows, D), BF16),
            jax.ShapeDtypeStruct((rows, D), BF16),
            jax.ShapeDtypeStruct((FIRST, D, D), BF16),
        ),
        in_specs=[pl.BlockSpec(memory_space=pltpu.HBM)] * 4,
        out_specs=(vmem,) * 3,
        scratch_shapes=[
            pltpu.VMEM((rows, D), BF16),
            pltpu.VMEM((1, rows), jnp.int32),
            pltpu.SemaphoreType.DMA((FIRST + 2,)),
        ],
        compiler_params=pltpu.CompilerParams(vmem_limit_bytes=20 << 20),
        cost_estimate=pl.CostEstimate(
            flops=2 * rows * rows * D, bytes_accessed=4 << 20, transcendentals=0
        ),
    )(*args)


def with_weights(block, own, came, body):
    section = lax.axis_index("section")

    @pl.when(section == block)
    def _():
        body(*own)

    @pl.when(section != block)
    def _():
        body(*came)


def turned(values, patch, pair):
    part = values[patch * PATCH : (patch + 1) * PATCH, pair * 128 : (pair + 1) * 128]
    return part.T.astype(BF16)


def prepare_kernel(block, sent, own, came, queries, keys, values):
    low = lax.broadcasted_iota(jnp.int32, (PATCH, 128), 1) < HEAD
    scale = jnp.asarray(HEAD**-0.5, BF16)
    low_scale = jnp.where(low, scale, 0.0).astype(BF16)
    high_scale = jnp.where(low, 0.0, scale).astype(BF16)

    def body(weights):
        normed = sent[...]
        query = dot(normed, weights[QKV]).astype(BF16)
        keys[...] = dot(normed, weights[QKV + 1]).astype(BF16)
        value = dot(normed, weights[QKV + 2])
        for patch in range(sent.shape[0] // PATCH):
            for pair in range(PAIRS):
                part = query[patch * PATCH : (patch + 1) * PATCH, pair * 128 : (pair + 1) * 128]
                queries[patch, pair, 0:PATCH, :] = part * low_scale
                queries[patch, pair, PATCH : 2 * PATCH, :] = part * high_scale
                values[patch, pair] = turned(value, patch, pair)

    with_weights(block, (own,), (came,), body)


def prepare(block, sent, own, came):
    rows = sent.shape[0]
    patches = rows // PATCH
    vmem = pl.BlockSpec(memory_space=pltpu.VMEM)
    return pl.pallas_call(
        functools.partial(prepare_kernel, block),
        out_shape=(
            jax.ShapeDtypeStruct((patches, PAIRS, 2 * PATCH, 128), BF16),
            jax.ShapeDtypeStruct((rows, D), BF16),
            jax.ShapeDtypeStruct((patches, PAIRS, 128, PATCH), BF16),
        ),
        in_specs=[vmem] * 3,
        out_specs=(vmem,) * 3,
        compiler_params=pltpu.CompilerParams(vmem_limit_bytes=LIMIT),
        cost_estimate=pl.CostEstimate(
            flops=6 * rows * D * D, bytes_accessed=4 << 20, transcendentals=0
        ),
    )(sent, own, came)


def attend_kernel(
    block,
    links_in,
    counts_in,
    state,
    queries,
    own_keys,
    own_values,
    near_a,
    near_b,
    own,
    came,
    middle,
    keys,
    values,
    scores,
    tops,
    totals,
    attended,
    links,
    counts,
    sem,
):
    event = lax.axis_index("section")
    region = lax.axis_index("region")
    regions = counts.shape[1]
    rows = state.shape[0]
    patches = rows // PATCH
    bring = copies_of(
        [
            (links_in, links),
            (counts_in, counts),
            (own_keys, keys.at[pl.ds(0, rows)]),
            (own_values, values.at[pl.ds(0, patches)]),
        ],
        sem,
    )
    for copy in bring:
        copy.start()
    even = lax.rem(region, 2) == 0
    region_a = jnp.where(even, region + 1, region - 1)
    region_b = jnp.where(even, region - 1, region + 1)
    key_row = lax.broadcasted_iota(jnp.int32, (PATCH, 2 * PATCH), 0)
    ones = jnp.ones((16, LINKS * PATCH), BF16)

    def body(weights):
        normed = jnp.concatenate([near_a[...], near_b[...]], axis=0)
        value = dot(normed, weights[QKV + 2])
        for patch in range(2 * patches):
            for pair in range(PAIRS):
                values[patches + patch, pair] = turned(value, patch, pair)
        keys[rows : 3 * rows, :] = dot(normed, weights[QKV + 1]).astype(BF16)
        for copy in bring:
            copy.wait()
        count_own = counts[event, region]
        count_a = counts[event, jnp.clip(region_a, 0, regions - 1)]
        count_b = counts[event, jnp.clip(region_b, 0, regions - 1)]
        slots = []
        for patch in range(patches):
            valid = []
            for link in range(LINKS):
                linked = links[event, patch, link]
                owner = lax.div(linked, patches)
                half = lax.rem(linked, patches)
                base = jnp.where(owner == region, 0, jnp.where(owner == region_a, 1, 2))
                count = jnp.where(base == 0, count_own, jnp.where(base == 1, count_a, count_b))
                slots.append(base * patches + half)
                valid.append(key_row < count - half * PATCH)
            for pair in range(PAIRS):
                unit = patch * PAIRS + pair
                query = queries[patch, pair]
                top = None
                for link in range(LINKS):
                    start = pl.multiple_of(slots[patch * LINKS + link] * PATCH, PATCH)
                    score = lax.dot_general(
                        keys[pl.ds(start, PATCH), pair * 128 : (pair + 1) * 128],
                        query,
                        (((1,), (1,)), ((), ())),
                        preferred_element_type=F32,
                    )
                    score = jnp.where(valid[link], score, -1e30)
                    scores[unit, link * PATCH : (link + 1) * PATCH, :] = score
                    top = score if top is None else jnp.maximum(top, score)
                tops[unit] = jnp.broadcast_to(jnp.max(top, axis=0, keepdims=True), (8, 2 * PATCH))
        for patch in range(patches):
            for pair in range(PAIRS):
                unit = patch * PAIRS + pair
                weighed = jnp.exp(scores[unit] - tops[unit, 0:1, :]).astype(BF16)
                taken = jnp.concatenate(
                    [values[slot, pair] for slot in slots[patch * LINKS : (patch + 1) * LINKS]],
                    axis=1,
                )
                totals[unit] = dot(jnp.concatenate([taken, ones], axis=0), weighed)
        for patch in range(patches):
            for pair in range(PAIRS):
                unit = patch * PAIRS + pair
                share = 1.0 / totals[unit, 128:129, :]
                whole = jnp.concatenate(
                    [
                        totals[unit, 0:HEAD, 0:PATCH] * share[:, 0:PATCH],
                        totals[unit, HEAD:128, PATCH:] * share[:, PATCH:],
                    ],
                    axis=0,
                )
                attended[
                    patch * PATCH : (patch + 1) * PATCH, pair * 128 : (pair + 1) * 128
                ] = whole.T.astype(BF16)
        middle[...] = (state[...].astype(F32) + dot(attended[...], weights[OUT])).astype(BF16)

    with_weights(block, (own,), (came,), body)


def attend(block, links, counts, state, queries, keys, values, near_a, near_b, own, came):
    rows = state.shape[0]
    patches = rows // PATCH
    vmem = pl.BlockSpec(memory_space=pltpu.VMEM)
    any_space = pl.BlockSpec(memory_space=pl.ANY)
    return pl.pallas_call(
        functools.partial(attend_kernel, block),
        out_shape=jax.ShapeDtypeStruct((rows, D), BF16),
        in_specs=[any_space] * 2 + [vmem] * 2 + [any_space] * 2 + [vmem] * 4,
        out_specs=vmem,
        scratch_shapes=[
            pltpu.VMEM((3 * rows, D), BF16),
            pltpu.VMEM((3 * patches, PAIRS, 128, PATCH), BF16),
            pltpu.VMEM((patches * PAIRS, LINKS * PATCH, 2 * PATCH), F32),
            pltpu.VMEM((patches * PAIRS, 8, 2 * PATCH), F32),
            pltpu.VMEM((patches * PAIRS, 144, 2 * PATCH), F32),
            pltpu.VMEM((rows, D), BF16),
            pltpu.SMEM(links.shape, jnp.int32),
            pltpu.SMEM(counts.shape, jnp.int32),
            pltpu.SemaphoreType.DMA((4,)),
        ],
        compiler_params=pltpu.CompilerParams(vmem_limit_bytes=LIMIT),
        cost_estimate=pl.CostEstimate(
            flops=10**9, bytes_accessed=4 << 20, transcendentals=8 * 10**5
        ),
    )(links, counts, state, queries, keys, values, near_a, near_b, own, came)


def raise_kernel(block, middle, own, came, hidden):
    def body(up):
        normed = normalize(middle[...].astype(F32))
        for part in range(0, FF, WIDTH):
            here = slice(part, part + WIDTH)
            hidden[:, here] = gelu(dot(normed, up[0, :, here])).astype(BF16)

    with_weights(block, (own,), (came,), body)


def lower_kernel(block, hidden, middle, own, came, result, sent):
    def body(down):
        total = (middle[...].astype(F32) + dot(hidden[...], down[0])).astype(BF16)
        result[...] = total
        sent[...] = normalize(total.astype(F32))

    with_weights(block, (own,), (came,), body)


def feed_kernel(
    block, counts_in, middle_ref, up_own, down_own, up_came, down_came, result, counts, sem
):
    bring = pltpu.make_async_copy(counts_in, counts, sem)
    bring.start()

    def body(up, down):
        middle = middle_ref[...].astype(F32)
        normed = normalize(middle)
        total = middle
        for part in range(0, FF, WIDTH):
            hidden = gelu(dot(normed, up[0, :, part : part + WIDTH])).astype(BF16)
            total = total + dot(hidden, down[0, part : part + WIDTH, :])
        bring.wait()
        count = counts[lax.axis_index("section"), lax.axis_index("region")]
        row = lax.broadcasted_iota(jnp.int32, total.shape, 0)
        result[...] = jnp.where(row < count, total, 0.0).astype(BF16)

    with_weights(block, (up_own, down_own), (up_came, down_came), body)


def feed_parts(block, middle, up_own, down_own, up_came, down_came):
    rows = middle.shape[0]
    vmem = pl.BlockSpec(memory_space=pltpu.VMEM)
    params = pltpu.CompilerParams(vmem_limit_bytes=LIMIT)
    cost = pl.CostEstimate(
        flops=2 * rows * FF * D, bytes_accessed=3 << 20, transcendentals=5 * 10**5
    )
    hidden = pl.pallas_call(
        functools.partial(raise_kernel, block),
        out_shape=jax.ShapeDtypeStruct((rows, FF), BF16),
        in_specs=[vmem] * 3,
        out_specs=vmem,
        compiler_params=params,
        cost_estimate=cost,
    )(middle, up_own, up_came)
    return pl.pallas_call(
        functools.partial(lower_kernel, block),
        out_shape=(jax.ShapeDtypeStruct((rows, D), BF16),) * 2,
        in_specs=[vmem] * 4,
        out_specs=(vmem,) * 2,
        compiler_params=params,
        cost_estimate=cost,
    )(hidden, middle, down_own, down_came)


def feed(block, counts, middle, *weights):
    rows = middle.shape[0]
    vmem = pl.BlockSpec(memory_space=pltpu.VMEM)
    return pl.pallas_call(
        functools.partial(feed_kernel, block),
        out_shape=jax.ShapeDtypeStruct((rows, D), BF16),
        in_specs=[pl.BlockSpec(memory_space=pl.ANY)] + [vmem] * 5,
        out_specs=vmem,
        scratch_shapes=[pltpu.SMEM(counts.shape, jnp.int32), pltpu.SemaphoreType.DMA],
        compiler_params=pltpu.CompilerParams(vmem_limit_bytes=LIMIT),
        cost_estimate=pl.CostEstimate(
            flops=4 * rows * FF * D, bytes_accessed=5 << 20, transcendentals=10**6
        ),
    )(counts, middle, *weights)


def per_device(hits, order, links, counts, w_qkv, w_out, w_up, w_down):
    regions = counts.shape[1]
    pairs_a = [(i, i ^ 1) for i in range(regions)]
    pairs_b = []
    for i in range(1, regions - 1, 2):
        pairs_b += [(i, i + 1), (i + 1, i)]
    swap = [(0, 1), (1, 0)]
    state, sent, own = arrange(hits, order, w_qkv, w_out)
    for block in range(2):
        near_b = lax.ppermute(sent, "region", pairs_b)
        if block == 0:
            came = lax.ppermute(own, "section", swap)
        near_a = lax.ppermute(sent, "region", pairs_a)
        if block == 0:
            up_came = lax.ppermute(w_up, "section", swap)
            down_came = lax.ppermute(w_down, "section", swap)
            second = (w_up, w_down, up_came, down_came)
        queries, keys, values = prepare(block, sent, own, came)
        middle = attend(
            block,
            links,
            counts,
            state,
            queries,
            keys,
            values,
            near_a,
            near_b,
            own,
            came,
        )
        if block == 0:
            state, sent = feed_parts(block, middle, *second)
        else:
            state = feed(block, counts, middle, *second)
    return state[None]


def solution(mesh):
    in_specs = (
        P("section", "region", None),
        P(None, "region", None),
        P(None, "region", None),
        P(),
        P("section", None, None),
        P("section", None, None),
        P("section", None, None),
        P("section", None, None),
    )
    out_specs = P("section", "region", None)
    return jax.shard_map(
        per_device, mesh=mesh, in_specs=in_specs, out_specs=out_specs, check_vma=False
    )
```

```python
import functools
import math

import jax
import jax.numpy as jnp
from jax import lax
from jax.experimental import pallas as pl
from jax.experimental.pallas import tpu as pltpu
from jax.sharding import PartitionSpec as P


HEADS = 8
HEAD = 64
D = 512
PATCH = 128
LINKS = 3
PAIRS = HEADS // 2
EPS = 1e-05
FF = 2048
WIDTH = 1024
LIMIT = 16 << 20
SCALE = HEAD**-0.5 * math.log2(math.e)
BF16 = jnp.bfloat16
F32 = jnp.float32

QKV, OUT, FIRST = 0, 3, 4


def dot(a, b):
    return jnp.dot(a, b, preferred_element_type=F32)


def normalize(values):
    center = jnp.mean(values, axis=-1, keepdims=True)
    shifted = values - center
    spread = jnp.mean(shifted * shifted, axis=-1, keepdims=True)
    return (shifted * lax.rsqrt(spread + EPS)).astype(BF16)


def gelu(x):
    return 0.5 * x * (1.0 + lax.erf(x * (0.5**0.5)))


def copies_of(pairs, sem):
    return [pltpu.make_async_copy(a, b, sem.at[i]) for i, (a, b) in enumerate(pairs)]


def arrange_kernel(hits_hbm, order_hbm, w_qkv, w_out, ordered, sent, packed, hits, order, sem):
    event = lax.axis_index("section")
    pairs = [(order_hbm.at[event], order), (hits_hbm.at[0], hits)]
    for i in range(3):
        pairs.append((w_qkv.at[0, :, pl.ds(i * D, D)], packed.at[QKV + i]))
    pairs.append((w_out.at[0], packed.at[OUT]))
    copies = copies_of(pairs, sem)
    for copy in copies:
        copy.start()
    rows = hits.shape[0]
    source_row = lax.broadcasted_iota(jnp.int32, (rows, rows), 0)
    copies[0].wait()
    chosen = jnp.where(source_row == order[...], 1.0, 0.0).T.astype(BF16)
    copies[1].wait()
    state = dot(chosen, hits[...]).astype(BF16)
    ordered[...] = state
    sent[...] = normalize(state.astype(F32))
    for copy in copies[2:]:
        copy.wait()


def arrange(hits, order, w_qkv, w_out):
    rows = hits.shape[1]
    vmem = pl.BlockSpec(memory_space=pltpu.VMEM)
    args = [pltpu.with_memory_space_constraint(a, pltpu.HBM) for a in (hits, order, w_qkv, w_out)]
    return pl.pallas_call(
        arrange_kernel,
        name="arrange",
        out_shape=(
            jax.ShapeDtypeStruct((rows, D), BF16),
            jax.ShapeDtypeStruct((rows, D), BF16),
            jax.ShapeDtypeStruct((FIRST, D, D), BF16),
        ),
        in_specs=[pl.BlockSpec(memory_space=pltpu.HBM)] * 4,
        out_specs=(vmem,) * 3,
        scratch_shapes=[
            pltpu.VMEM((rows, D), BF16),
            pltpu.VMEM((1, rows), jnp.int32),
            pltpu.SemaphoreType.DMA((FIRST + 2,)),
        ],
        compiler_params=pltpu.CompilerParams(vmem_limit_bytes=20 << 20),
        cost_estimate=pl.CostEstimate(
            flops=2 * rows * rows * D, bytes_accessed=4 << 20, transcendentals=0
        ),
    )(*args)


def with_weights(block, own, came, body):
    section = lax.axis_index("section")

    @pl.when(section == block)
    def _():
        body(*own)

    @pl.when(section != block)
    def _():
        body(*came)


def match(key, query):
    return lax.dot_general(key, query, (((1,), (1,)), ((), ())), preferred_element_type=F32)


def turned(values, patch, pair):
    part = values[patch * PATCH : (patch + 1) * PATCH, pair * 128 : (pair + 1) * 128]
    return part.T.astype(BF16)


def prepare_kernel(
    block, counts_in, sent, own, came, queries, keys, values, scores, tops, counts, sem
):
    bring = pltpu.make_async_copy(counts_in, counts, sem)
    bring.start()
    low = lax.broadcasted_iota(jnp.int32, (PATCH, 128), 1) < HEAD
    key_row = lax.broadcasted_iota(jnp.int32, (PATCH, 2 * PATCH), 0)
    patches = sent.shape[0] // PATCH

    def body(weights):
        normed = sent[...]
        query = dot(normed, weights[QKV]) * SCALE
        for patch in range(patches):
            for pair in range(PAIRS):
                part = query[patch * PATCH : (patch + 1) * PATCH, pair * 128 : (pair + 1) * 128]
                queries[patch, pair, 0:PATCH, :] = jnp.where(low, part, 0.0).astype(BF16)
                queries[patch, pair, PATCH : 2 * PATCH, :] = jnp.where(low, 0.0, part).astype(BF16)
        keys[...] = dot(normed, weights[QKV + 1]).astype(BF16)
        value = dot(normed, weights[QKV + 2])
        bring.wait()
        count = counts[lax.axis_index("section"), lax.axis_index("region")]
        for patch in range(patches):
            valid = key_row < count - patch * PATCH
            for pair in range(PAIRS):
                unit = patch * PAIRS + pair
                across = slice(pair * 128, (pair + 1) * 128)
                score = match(keys[patch * PATCH : (patch + 1) * PATCH, across], queries[patch, pair])
                score = jnp.where(valid, score, -1e30)
                scores[unit] = score
                tops[unit] = jnp.broadcast_to(jnp.max(score, axis=0, keepdims=True), (8, 2 * PATCH))
                values[patch, pair] = turned(value, patch, pair)

    with_weights(block, (own,), (came,), body)


def prepare(block, counts, sent, own, came):
    rows = sent.shape[0]
    patches = rows // PATCH
    units = patches * PAIRS
    vmem = pl.BlockSpec(memory_space=pltpu.VMEM)
    return pl.pallas_call(
        functools.partial(prepare_kernel, block),
        out_shape=(
            jax.ShapeDtypeStruct((patches, PAIRS, 2 * PATCH, 128), BF16),
            jax.ShapeDtypeStruct((rows, D), BF16),
            jax.ShapeDtypeStruct((patches, PAIRS, 128, PATCH), BF16),
            jax.ShapeDtypeStruct((units, PATCH, 2 * PATCH), F32),
            jax.ShapeDtypeStruct((units, 8, 2 * PATCH), F32),
        ),
        in_specs=[pl.BlockSpec(memory_space=pl.ANY)] + [vmem] * 3,
        out_specs=(vmem,) * 5,
        scratch_shapes=[pltpu.SMEM(counts.shape, jnp.int32), pltpu.SemaphoreType.DMA],
        compiler_params=pltpu.CompilerParams(vmem_limit_bytes=LIMIT),
        cost_estimate=pl.CostEstimate(
            flops=7 * rows * D * D, bytes_accessed=4 << 20, transcendentals=0
        ),
    )(counts, sent, own, came)


def attend_kernel(
    block,
    links_in,
    counts_in,
    state,
    queries,
    own_keys,
    own_values,
    own_scores,
    own_tops,
    near_a,
    near_b,
    own,
    came,
    middle,
    keys,
    values,
    scores,
    tops,
    totals,
    attended,
    links,
    counts,
    sem,
):
    event = lax.axis_index("section")
    region = lax.axis_index("region")
    regions = counts.shape[1]
    rows = state.shape[0]
    patches = rows // PATCH
    bring = copies_of([(links_in, links), (counts_in, counts)], sem)
    for copy in bring:
        copy.start()
    even = lax.rem(region, 2) == 0
    region_a = jnp.where(even, region + 1, region - 1)
    region_b = jnp.where(even, region - 1, region + 1)
    key_row = lax.broadcasted_iota(jnp.int32, (PATCH, 2 * PATCH), 0)
    ones = jnp.ones((16, LINKS * PATCH), BF16)

    def body(weights):
        normed = jnp.concatenate([near_a[...], near_b[...]], axis=0)
        value = dot(normed, weights[QKV + 2])
        for patch in range(2 * patches):
            for pair in range(PAIRS):
                values[patches + patch, pair] = turned(value, patch, pair)
        keys[rows : 3 * rows, :] = dot(normed, weights[QKV + 1]).astype(BF16)
        keys[0:rows, :] = own_keys[...]
        values[0:patches] = own_values[...]
        for copy in bring:
            copy.wait()
        count_own = counts[event, region]
        count_a = counts[event, jnp.clip(region_a, 0, regions - 1)]
        count_b = counts[event, jnp.clip(region_b, 0, regions - 1)]
        slots = []
        for patch in range(patches):
            valid = []
            for link in range(1, LINKS):
                linked = links[event, patch, link]
                owner = jnp.right_shift(linked, 1)
                half = jnp.bitwise_and(linked, 1)
                base = jnp.where(owner == region, 0, jnp.where(owner == region_a, 1, 2))
                count = jnp.where(base == 0, count_own, jnp.where(base == 1, count_a, count_b))
                slots.append(base * patches + half)
                valid.append(key_row < count - half * PATCH)
            for pair in range(PAIRS):
                unit = patch * PAIRS + pair
                query = queries[patch, pair]
                top = None
                for link in range(1, LINKS):
                    start = pl.multiple_of(slots[patch * (LINKS - 1) + link - 1] * PATCH, PATCH)
                    key = keys[pl.ds(start, PATCH), pair * 128 : (pair + 1) * 128]
                    score = jnp.where(valid[link - 1], match(key, query), -1e30)
                    scores[unit, (link - 1) * PATCH : link * PATCH, :] = score
                    top = score if top is None else jnp.maximum(top, score)
                top = jnp.broadcast_to(jnp.max(top, axis=0, keepdims=True), (8, 2 * PATCH))
                tops[unit] = jnp.maximum(top, own_tops[unit])
        for patch in range(patches):
            for pair in range(PAIRS):
                unit = patch * PAIRS + pair
                top = tops[unit, 0:1, :]
                near_slots = slots[patch * (LINKS - 1) : (patch + 1) * (LINKS - 1)]
                weighed = jnp.concatenate(
                    [
                        jnp.exp2(own_scores[unit] - top).astype(BF16),
                        jnp.exp2(scores[unit] - top).astype(BF16),
                    ],
                    axis=0,
                )
                taken = jnp.concatenate(
                    [own_values[patch, pair]]
                    + [values[slot, pair] for slot in near_slots],
                    axis=1,
                )
                totals[unit] = dot(jnp.concatenate([taken, ones], axis=0), weighed)
        for patch in range(patches):
            for pair in range(PAIRS):
                unit = patch * PAIRS + pair
                share = 1.0 / totals[unit, 128:129, :]
                whole = jnp.concatenate(
                    [
                        totals[unit, 0:HEAD, 0:PATCH] * share[:, 0:PATCH],
                        totals[unit, HEAD:128, PATCH:] * share[:, PATCH:],
                    ],
                    axis=0,
                )
                attended[
                    patch * PATCH : (patch + 1) * PATCH, pair * 128 : (pair + 1) * 128
                ] = whole.T.astype(BF16)
        middle[...] = (state[...].astype(F32) + dot(attended[...], weights[OUT])).astype(BF16)

    with_weights(block, (own,), (came,), body)


def attend(block, links, counts, state, prepared, near_a, near_b, own, came):
    rows = state.shape[0]
    patches = rows // PATCH
    vmem = pl.BlockSpec(memory_space=pltpu.VMEM)
    any_space = pl.BlockSpec(memory_space=pl.ANY)
    return pl.pallas_call(
        functools.partial(attend_kernel, block),
        out_shape=jax.ShapeDtypeStruct((rows, D), BF16),
        in_specs=[any_space] * 2 + [vmem] * 10,
        out_specs=vmem,
        scratch_shapes=[
            pltpu.VMEM((3 * rows, D), BF16),
            pltpu.VMEM((3 * patches, PAIRS, 128, PATCH), BF16),
            pltpu.VMEM((patches * PAIRS, (LINKS - 1) * PATCH, 2 * PATCH), F32),
            pltpu.VMEM((patches * PAIRS, 8, 2 * PATCH), F32),
            pltpu.VMEM((patches * PAIRS, 144, 2 * PATCH), F32),
            pltpu.VMEM((rows, D), BF16),
            pltpu.SMEM(links.shape, jnp.int32),
            pltpu.SMEM(counts.shape, jnp.int32),
            pltpu.SemaphoreType.DMA((2,)),
        ],
        compiler_params=pltpu.CompilerParams(vmem_limit_bytes=LIMIT),
        cost_estimate=pl.CostEstimate(
            flops=10**9, bytes_accessed=4 << 20, transcendentals=8 * 10**5
        ),
    )(links, counts, state, *prepared, near_a, near_b, own, came)


def raise_kernel(block, middle, own, came, hidden):
    def body(up):
        normed = normalize(middle[...].astype(F32))
        for part in range(0, FF, WIDTH):
            here = slice(part, part + WIDTH)
            hidden[:, here] = gelu(dot(normed, up[0, :, here])).astype(BF16)

    with_weights(block, (own,), (came,), body)


def lower_kernel(block, hidden, middle, own, came, result, sent):
    def body(down):
        total = (middle[...].astype(F32) + dot(hidden[...], down[0])).astype(BF16)
        result[...] = total
        sent[...] = normalize(total.astype(F32))

    with_weights(block, (own,), (came,), body)


def feed_kernel(
    block, counts_in, middle_ref, up_own, down_own, up_came, down_came, result, counts, sem
):
    bring = pltpu.make_async_copy(counts_in, counts, sem)
    bring.start()

    def body(up, down):
        middle = middle_ref[...].astype(F32)
        normed = normalize(middle)
        total = middle
        for part in range(0, FF, WIDTH):
            hidden = gelu(dot(normed, up[0, :, part : part + WIDTH])).astype(BF16)
            total = total + dot(hidden, down[0, part : part + WIDTH, :])
        bring.wait()
        count = counts[lax.axis_index("section"), lax.axis_index("region")]
        row = lax.broadcasted_iota(jnp.int32, total.shape, 0)
        result[...] = jnp.where(row < count, total, 0.0).astype(BF16)

    with_weights(block, (up_own, down_own), (up_came, down_came), body)


def feed_parts(block, middle, up_own, down_own, up_came, down_came):
    rows = middle.shape[0]
    vmem = pl.BlockSpec(memory_space=pltpu.VMEM)
    params = pltpu.CompilerParams(vmem_limit_bytes=LIMIT)
    cost = pl.CostEstimate(
        flops=2 * rows * FF * D, bytes_accessed=3 << 20, transcendentals=5 * 10**5
    )
    hidden = pl.pallas_call(
        functools.partial(raise_kernel, block),
        out_shape=jax.ShapeDtypeStruct((rows, FF), BF16),
        in_specs=[vmem] * 3,
        out_specs=vmem,
        compiler_params=params,
        cost_estimate=cost,
    )(middle, up_own, up_came)
    return pl.pallas_call(
        functools.partial(lower_kernel, block),
        out_shape=(jax.ShapeDtypeStruct((rows, D), BF16),) * 2,
        in_specs=[vmem] * 4,
        out_specs=(vmem,) * 2,
        compiler_params=params,
        cost_estimate=cost,
    )(hidden, middle, down_own, down_came)


def feed(block, counts, middle, *weights):
    rows = middle.shape[0]
    vmem = pl.BlockSpec(memory_space=pltpu.VMEM)
    return pl.pallas_call(
        functools.partial(feed_kernel, block),
        out_shape=jax.ShapeDtypeStruct((rows, D), BF16),
        in_specs=[pl.BlockSpec(memory_space=pl.ANY)] + [vmem] * 5,
        out_specs=vmem,
        scratch_shapes=[pltpu.SMEM(counts.shape, jnp.int32), pltpu.SemaphoreType.DMA],
        compiler_params=pltpu.CompilerParams(vmem_limit_bytes=LIMIT),
        cost_estimate=pl.CostEstimate(
            flops=4 * rows * FF * D, bytes_accessed=5 << 20, transcendentals=10**6
        ),
    )(counts, middle, *weights)


def per_device(hits, order, links, counts, w_qkv, w_out, w_up, w_down):
    regions = counts.shape[1]
    pairs_a = [(i, i ^ 1) for i in range(regions)]
    pairs_b = []
    for i in range(1, regions - 1, 2):
        pairs_b += [(i, i + 1), (i + 1, i)]
    swap = [(0, 1), (1, 0)]
    state, sent, own = arrange(hits, order, w_qkv, w_out)
    for block in range(2):
        near_b = lax.ppermute(sent, "region", pairs_b)
        if block == 0:
            came = lax.ppermute(own, "section", swap)
        near_a = lax.ppermute(sent, "region", pairs_a)
        if block == 0:
            up_came = lax.ppermute(w_up, "section", swap)
            down_came = lax.ppermute(w_down, "section", swap)
            second = (w_up, w_down, up_came, down_came)
        prepared = prepare(block, counts, sent, own, came)
        middle = attend(block, links, counts, state, prepared, near_a, near_b, own, came)
        if block == 0:
            state, sent = feed_parts(block, middle, *second)
        else:
            state = feed(block, counts, middle, *second)
    return state[None]


def solution(mesh):
    in_specs = (
        P("section", "region", None),
        P(None, "region", None),
        P(None, "region", None),
        P(),
        P("section", None, None),
        P("section", None, None),
        P("section", None, None),
        P("section", None, None),
    )
    out_specs = P("section", "region", None)
    return jax.shard_map(
        per_device, mesh=mesh, in_specs=in_specs, out_specs=out_specs, check_vma=False
    )
```
